1024 devices in a mesh: dp: 16 (over z_lo, core), ctx: 64 (over y, x, z_hi).
Axes of the slice: x: 4, y: 8, z: 16 (z_hi: 2, z_lo: 8; z = z_hi * 8 + z_lo), core: 2. Of those that a mesh axis runs over, the one named last changes fastest.
Arguments:
- queries: bfloat16 [16, 8192, 2048], P('dp', 'ctx'), may hold values from -150 to 150
- key_rows: bfloat16 [16, 8192, 512], P('dp', 'ctx'), may hold values from -5 to 5
- value_rows: bfloat16 [16, 8192, 512], P('dp', 'ctx'), may hold values from -6 to 6
- cotangent: bfloat16 [16, 8192, 2048], P('dp', 'ctx'), may hold values from -6 to 6
- sink_logits: float32 [16], replicated, may hold values from -1 to 3
- run_lengths: int32 [16, 16], P('dp'), may hold values from 1 to 8, 64 in all within a row
- segment_ids: int32 [16, 8192], P('dp', 'ctx'), may hold values from 0 to 15, never falling along the last dimension, each value on 1 to 1024 neighbouring positions
Outputs:
- attended: bfloat16 [16, 8192, 2048], P('dp', 'ctx')
- grad_queries: bfloat16 [16, 8192, 2048], P('dp', 'ctx')
- grad_keys: bfloat16 [16, 8192, 512], P('dp', 'ctx')
- grad_values: bfloat16 [16, 8192, 512], P('dp', 'ctx')
- grad_sink: float32 [16], replicated
The draws below stay inside these ranges and needn't reach their ends.
Inputs may be any that keep to these rules, and one draw needn't show every extreme that they name: `run_lengths`: in each sequence the trajectories cover all shards in order; each spans 1 to 8 shards and one spans exactly 8. `segment_ids`: never falls along a sequence; each episode spans 1 to 1024 tokens and one spans exactly 1024.
All inputs are finite; a program needn't handle non-finite values.
Results may differ from the reference program's by a relative error of at most 0.04.
Values may be sent and summed in bfloat16 or wider, within the bound.
No kernel may reach another device: no remote copies, remote signals or barrier semaphores. Data moves between devices by JAX's collectives and lax.ppermute only.
A program may use at most 64 MiB of HBM per device.

```python
import math
import jax
import jax.numpy as jnp
import numpy as np
from jax import lax

HEADS = 16
KV_HEADS = 4
HEAD_DIM = 128
TOK_DEV = 128
BATCH = 16
SEQ = 8192
MOST = 8
RUNS = 16
SEG_MOST = 1024
SEG_COUNT = 16
N_CTX = 64


def draw_key_rows(key, part):
    drawn_draw = jax.random.normal(jax.random.fold_in(key, 21), (BATCH, SEQ, KV_HEADS * HEAD_DIM), jnp.float32)
    return jnp.clip(drawn_draw, -5.0, 5.0).astype(jnp.bfloat16)


def draw_queries(key, part):
    group_size = HEADS // KV_HEADS
    base_draw = jnp.clip(jax.random.normal(jax.random.fold_in(key, 31), (BATCH, SEQ, KV_HEADS, group_size, HEAD_DIM), jnp.float32), -5.0, 5.0)
    return base_draw.reshape(BATCH, SEQ, HEADS * HEAD_DIM).astype(jnp.bfloat16)


def shard_levels(rng, shape, cuts, low, high):
    gain = 1.0
    for position, parts in cuts:
        draws = jax.random.uniform(jax.random.fold_in(jax.random.fold_in(rng, 6), position), (parts,), jnp.float32, low / len(cuts), high / len(cuts))
        gain = gain * jnp.repeat(jnp.exp(draws), shape[position] // parts).reshape((-1,) + (1,) * (len(shape) - 1 - position))
    return gain


def split_up(count, total, limit, slope):
    weights = [(1 << 20) // math.isqrt(standing ** slope) + 1 for standing in range(2, count + 1)]
    rest, given = total - limit - (count - 1), [1] * (count - 1)
    while rest > 0:
        free = [i for i in range(count - 1) if given[i] < limit]
        mass, left = sum([weights[i] for i in free]), rest
        for i in free:
            addition = min(limit - given[i], max(1, left * weights[i] // mass), rest)
            given[i] = given[i] + addition
            rest = rest - addition
    return np.array([limit] + given)


def uneven(key, amount, total, bound, skew):
    if amount == 2:
        one = jax.random.randint(key, (), max(1, total - bound), min(bound, total - 1) + 1)
        return jnp.stack([one, total - one])
    sizes = jnp.asarray(split_up(amount, total, bound, skew), jnp.int32)
    pairs = (amount - 1) // 2
    giver, sink = sizes[1:1 + 2 * pairs:2], sizes[2:2 + 2 * pairs:2]
    room = jnp.minimum(giver - 1, bound - sink)
    moved = jax.random.randint(jax.random.fold_in(key, 1), (pairs,), 0, 1 << 20) % (room + 1)
    sizes = sizes.at[1:1 + 2 * pairs:2].set(giver - moved).at[2:2 + 2 * pairs:2].set(sink + moved)
    return sizes[jax.random.permutation(jax.random.fold_in(key, 2), amount)]


def normal_values(key, shape, deviation, reach, pieces=(), kind=jnp.bfloat16):
    gain = shard_levels(key, shape, pieces, -0.22, 0.18) if pieces else 1.0
    entries = jax.random.normal(key, shape, jnp.float32) * deviation * gain
    return jnp.minimum(jnp.maximum(entries, -reach), reach).astype(kind)


def setup_inputs(seed: int = 0) -> dict:
    arg_keys = jax.random.split(jax.random.key(seed), 8)
    return {
        "queries": draw_queries(jax.random.fold_in(arg_keys[7], 71), 0),
        "key_rows": draw_key_rows(jax.random.fold_in(arg_keys[7], 71), 0),
        "value_rows": normal_values(arg_keys[2], (BATCH, SEQ, KV_HEADS * HEAD_DIM), 1.0, 6.0, ((0, 16), (1, 64))),
        "cotangent": normal_values(arg_keys[3], (BATCH, SEQ, HEADS * HEAD_DIM), 1.0, 6.0, ((0, 16), (1, 64))),
        "sink_logits": jnp.clip(jax.random.uniform(arg_keys[4], (HEADS,), jnp.float32, -1.0, 3.0), -1.0, 3.0),
        "run_lengths": jax.vmap(lambda own: uneven(own, RUNS, N_CTX, MOST, 2))(jax.random.split(arg_keys[5], BATCH)).reshape((BATCH, RUNS)).astype(jnp.int32),
        "segment_ids": jax.vmap(lambda own: jnp.searchsorted(jnp.cumsum(uneven(own, SEG_COUNT, SEQ, SEG_MOST, 2)), jnp.arange(SEQ), side="right"))(jax.random.split(arg_keys[6], BATCH)).reshape((BATCH, SEQ)).astype(jnp.int32),
    }


def traj_index(run_ends, shard_index):
    return lax.optimization_barrier(jnp.sum((run_ends[None, :] <= shard_index[:, None]).astype(jnp.int32), axis=1))

def head_block(query_heads, key_win, value_win, grad_heads, allowed, sink_part, factor):
    query_f = query_heads.astype(jnp.float32)
    key_f = key_win.astype(jnp.float32)
    value_f = value_win.astype(jnp.float32)
    grad_f = grad_heads.astype(jnp.float32)
    scores = jnp.einsum('rgd,wd->grw', query_f, key_f) * factor
    scores = jnp.where(allowed[None], scores, -jnp.inf)
    row_top = jnp.maximum(lax.optimization_barrier(jnp.max(scores, axis=2)), sink_part[:, None])
    exp_terms = jnp.exp(scores - row_top[:, :, None])
    sink_exp = jnp.exp(sink_part[:, None] - row_top)
    denominator = lax.optimization_barrier(jnp.sum(exp_terms, axis=2)) + sink_exp
    weights = exp_terms / denominator[:, :, None]
    weights_low = weights.astype(jnp.bfloat16)
    attended = jnp.einsum('grw,wd->rgd', weights_low.astype(jnp.float32), value_f).astype(jnp.bfloat16)
    row_dot = lax.optimization_barrier(jnp.sum(grad_f * attended.astype(jnp.float32), axis=2)).T
    grad_weights = jnp.einsum('rgd,wd->grw', grad_f, value_f)
    grad_scores = (weights * (grad_weights - row_dot[:, :, None])).astype(jnp.bfloat16)
    grad_scores_f = grad_scores.astype(jnp.float32)
    grad_query = (jnp.einsum('grw,wd->rgd', grad_scores_f, key_f) * factor).astype(jnp.bfloat16)
    grad_key = jnp.einsum('grw,rgd->wd', grad_scores_f, query_f) * factor
    grad_value = jnp.einsum('grw,rgd->wd', weights_low.astype(jnp.float32), grad_f)
    grad_sink = -lax.optimization_barrier(jnp.sum(sink_exp / denominator * row_dot, axis=1))
    return (attended, grad_query, grad_key, grad_value, grad_sink)

def reference(queries, key_rows, value_rows, cotangent, sink_logits, run_lengths, segment_ids):
    group_size = HEADS // KV_HEADS
    factor = HEAD_DIM ** (-0.5)
    pad_rows = (MOST - 1) * TOK_DEV
    span_rows = MOST * TOK_DEV
    kv_width = KV_HEADS * HEAD_DIM

    def one_sequence(packed):
        query_seq, key_seq, value_seq, grad_seq, lengths, seg_seq = packed
        run_ends = jnp.cumsum(lengths).astype(jnp.int32)
        key_pad = jnp.concatenate([jnp.zeros((pad_rows, kv_width), key_seq.dtype), key_seq], 0)
        value_pad = jnp.concatenate([jnp.zeros((pad_rows, kv_width), value_seq.dtype), value_seq], 0)
        seg_pad = jnp.concatenate([jnp.full((pad_rows,), -1, jnp.int32), seg_seq.astype(jnp.int32)], 0)

        def visit_shard(carried, shard_index):
            key_acc, value_acc = carried
            start_row = (shard_index * TOK_DEV).astype(jnp.int32)
            query_blk = lax.dynamic_slice_in_dim(query_seq, start_row, TOK_DEV, 0)
            grad_blk = lax.dynamic_slice_in_dim(grad_seq, start_row, TOK_DEV, 0)
            seg_query = lax.dynamic_slice_in_dim(seg_seq.astype(jnp.int32), start_row, TOK_DEV, 0)
            key_win = lax.dynamic_slice_in_dim(key_pad, start_row, span_rows, 0)
            value_win = lax.dynamic_slice_in_dim(value_pad, start_row, span_rows, 0)
            seg_win = lax.dynamic_slice_in_dim(seg_pad, start_row, span_rows, 0)
            columns = jnp.arange(span_rows, dtype=jnp.int32)
            key_shard = shard_index - MOST + 1 + columns // TOK_DEV
            key_pos = key_shard * TOK_DEV + columns % TOK_DEV
            query_pos = start_row + jnp.arange(TOK_DEV, dtype=jnp.int32)
            my_traj = jnp.sum((run_ends <= shard_index).astype(jnp.int32))
            allowed = ((key_shard >= 0) & (traj_index(run_ends, key_shard) == my_traj))[None, :] & (seg_win[None, :] == seg_query[:, None]) & (key_pos[None, :] <= query_pos[:, None])
            outs_list = [[], [], [], [], []]
            for kv_head in range(KV_HEADS):
                query_cols = slice(kv_head * group_size * HEAD_DIM, (kv_head + 1) * group_size * HEAD_DIM)
                key_cols = slice(kv_head * HEAD_DIM, (kv_head + 1) * HEAD_DIM)
                head_parts = head_block(query_blk[:, query_cols].reshape(TOK_DEV, group_size, HEAD_DIM), key_win[:, key_cols], value_win[:, key_cols], grad_blk[:, query_cols].reshape(TOK_DEV, group_size, HEAD_DIM), allowed, sink_logits[kv_head * group_size:(kv_head + 1) * group_size], factor)
                for member in range(5):
                    outs_list[member].append(head_parts[member])
            attended = jnp.concatenate([block_out.reshape(TOK_DEV, -1) for block_out in outs_list[0]], 1)
            grad_query = jnp.concatenate([block_out.reshape(TOK_DEV, -1) for block_out in outs_list[1]], 1)
            grad_key = jnp.concatenate(outs_list[2], 1)
            grad_value = jnp.concatenate(outs_list[3], 1)
            grad_sink = jnp.concatenate(outs_list[4], 0)
            key_old = lax.dynamic_slice_in_dim(key_acc, start_row, span_rows, 0).astype(jnp.float32)
            value_old = lax.dynamic_slice_in_dim(value_acc, start_row, span_rows, 0).astype(jnp.float32)
            key_acc = lax.dynamic_update_slice_in_dim(key_acc, (key_old + grad_key).astype(jnp.bfloat16), start_row, 0)
            value_acc = lax.dynamic_update_slice_in_dim(value_acc, (value_old + grad_value).astype(jnp.bfloat16), start_row, 0)
            return ((key_acc, value_acc), (attended, grad_query, grad_sink))
        zeros_acc = jnp.zeros((pad_rows + SEQ, kv_width), jnp.bfloat16)
        order = (N_CTX - 1 - jnp.arange(N_CTX, dtype=jnp.int32)).astype(jnp.int32)
        (key_acc, value_acc), (attended, grad_query, grad_sink) = lax.scan(visit_shard, (zeros_acc, zeros_acc), order)
        return (attended[::-1].reshape(SEQ, -1), grad_query[::-1].reshape(SEQ, -1), key_acc[pad_rows:], value_acc[pad_rows:], lax.optimization_barrier(jnp.sum(grad_sink, axis=0)))
    attended, grad_queries, grad_keys, grad_values, sink_parts = lax.map(one_sequence, (queries, key_rows, value_rows, cotangent, run_lengths, segment_ids))
    grad_sink = lax.optimization_barrier(jnp.sum(sink_parts, axis=0)) / math.sqrt(BATCH * SEQ)
    return (attended, grad_queries, grad_keys, grad_values, grad_sink)
```

```python
import math

import jax
import jax.numpy as jnp
from jax import lax
from jax.experimental import pallas as pl
from jax.experimental.pallas import tpu as pltpu
from jax.sharding import Mesh
from jax.sharding import PartitionSpec as P


HEADS = 16
KV_HEADS = 4
HEAD_DIM = 128
GROUP = HEADS // KV_HEADS
TOK = 128
MOST = 8
KV_COLS = KV_HEADS * HEAD_DIM
PACK_ROWS = 2 * TOK + 8
WIN = MOST * TOK
GROUP_COLS = GROUP * HEAD_DIM
FACTOR = HEAD_DIM ** (-0.5)
CTX = ("ctx_0", "ctx_1", "ctx_2")
DP = ("dp_0", "dp_1")


NT = (((1,), (1,)), ((), ()))
NN = (((1,), (0,)), ((), ()))


def passed_along(array, by):
    devices = lax.axis_size(CTX)
    pairs = [(i, i + by) for i in range(devices) if 0 <= i + by < devices]
    return lax.ppermute(array, CTX, pairs)


def dot(left, right, dims):
    return lax.dot_general(left, right, dims, preferred_element_type=jnp.float32)


def attention_kernel(
    marks_ref,
    sink_ref,
    bias_ref,
    query_ref,
    grad_ref,
    *refs,
):
    packs = refs[:MOST]
    (out_ref, grad_query_ref, near_ref, far2_ref, far4_ref, far6_ref, sink_grad_ref) = refs[
        MOST : MOST + 7
    ]
    mask_ref, score_ref, cross_ref, weight_ref, slope_ref = refs[MOST + 7 :]
    kv_head = pl.program_id(0)

    @pl.when(kv_head == 0)
    def _():
        mask_ref[:TOK, :] = bias_ref[...]
        rows = lax.broadcasted_iota(jnp.int32, (TOK, TOK), 0)
        cols = lax.broadcasted_iota(jnp.int32, (TOK, TOK), 1)
        reach = marks_ref[0]
        first_mark = marks_ref[1].astype(jnp.float32)
        first_count = marks_ref[2]
        for slot in range(1, MOST):
            row = packs[slot][2 * TOK : 2 * TOK + 8, :].astype(jnp.float32)[:1, :]
            same = jnp.sum((row == first_mark).astype(jnp.float32), axis=1, keepdims=True)
            same = jnp.where(slot <= reach, same, 0.0)
            seen = (rows >= TOK - same.astype(jnp.int32)) & (cols < first_count)
            mask_ref[slot * TOK : (slot + 1) * TOK, :] = jnp.where(seen, 0.0, -jnp.inf)

    def stacked(ref):
        return jnp.concatenate(
            [ref[:, g * HEAD_DIM : (g + 1) * HEAD_DIM] for g in range(GROUP)], axis=0
        )

    query = stacked(query_ref)
    grad = stacked(grad_ref)
    keys = jnp.concatenate([pack[:TOK, :] for pack in packs], axis=0)
    values = jnp.concatenate([pack[TOK : 2 * TOK, :] for pack in packs], axis=0)
    score_ref[...] = dot(keys, query, NT)
    cross_ref[...] = dot(values, grad, NT)
    blocks = [slice(slot * TOK, (slot + 1) * TOK) for slot in range(MOST)]
    lanes = [slice(g * TOK, (g + 1) * TOK) for g in range(GROUP)]
    sink_weights = []
    for g in range(GROUP):
        sink = sink_ref[kv_head * GROUP + g]
        best = jnp.full((8, TOK), sink, jnp.float32)
        for rows in blocks:
            scores = score_ref[rows, lanes[g]] * FACTOR + mask_ref[rows, :]
            score_ref[rows, lanes[g]] = scores
            best = jnp.maximum(best, jnp.max(scores.reshape(TOK // 8, 8, TOK), axis=0))
        top = jnp.max(best, axis=0, keepdims=True)
        total = jnp.zeros((8, TOK), jnp.float32)
        for rows in blocks:
            terms = jnp.exp(score_ref[rows, lanes[g]] - top)
            score_ref[rows, lanes[g]] = terms
            total = total + jnp.sum(terms.reshape(TOK // 8, 8, TOK), axis=0)
        sink_exp = jnp.exp(sink - top)
        scale = 1.0 / (jnp.sum(total, axis=0, keepdims=True) + sink_exp)
        for rows in blocks:
            weights = score_ref[rows, lanes[g]] * scale
            score_ref[rows, lanes[g]] = weights
            weight_ref[rows, lanes[g]] = weights.astype(jnp.bfloat16)
        sink_weights.append(sink_exp * scale)
    out_t = dot(values.T, weight_ref[...], NN).astype(jnp.bfloat16)
    grad_t = grad.T
    row_dot = jnp.sum(grad_t.astype(jnp.float32) * out_t.astype(jnp.float32), axis=0, keepdims=True)
    for g in range(GROUP):
        here = row_dot[:, lanes[g]]
        for rows in blocks:
            slope_ref[rows, lanes[g]] = (
                score_ref[rows, lanes[g]] * (cross_ref[rows, lanes[g]] - here)
            ).astype(jnp.bfloat16)
    sink_grad_ref[pl.ds(kv_head, 1), :] = jnp.concatenate(sink_weights, axis=1) * row_dot
    out = out_t.T
    grad_query = (dot(keys.T, slope_ref[...], NN) * FACTOR).astype(jnp.bfloat16).T
    for g in range(GROUP):
        cols = slice(g * HEAD_DIM, (g + 1) * HEAD_DIM)
        out_ref[:, cols] = out[lanes[g], :]
        grad_query_ref[:, cols] = grad_query[lanes[g], :]
    grad_key = dot(slope_ref[...], query, NN) * FACTOR
    grad_value = dot(weight_ref[...], grad, NN)
    for slot, (ref, half) in enumerate(
        [
            (near_ref, 0),
            (near_ref, 1),
            (far2_ref, 0),
            (far2_ref, 1),
            (far4_ref, 0),
            (far4_ref, 1),
            (far6_ref, 0),
            (far6_ref, 1),
        ]
    ):
        start = half * 2 * TOK
        ref[start : start + TOK, :] = grad_key[blocks[slot], :].astype(ref.dtype)
        ref[start + TOK : start + 2 * TOK, :] = grad_value[blocks[slot], :].astype(ref.dtype)


def attention(marks, sink_logits, bias, queries, cotangent, packs):
    wide = pl.BlockSpec((TOK, GROUP_COLS), lambda h: (0, h))
    pack_spec = pl.BlockSpec((PACK_ROWS, HEAD_DIM), lambda h: (0, h))
    pair_spec = pl.BlockSpec((4 * TOK, HEAD_DIM), lambda h: (0, h))
    smem = pl.BlockSpec(memory_space=pltpu.SMEM)
    pair_shape = (4 * TOK, KV_COLS)
    return pl.pallas_call(
        attention_kernel,
        grid=(KV_HEADS,),
        in_specs=[smem, smem, pl.BlockSpec((TOK, TOK), lambda h: (0, 0)), wide, wide]
        + [pack_spec] * MOST,
        out_specs=[
            wide,
            wide,
            pair_spec,
            pair_spec,
            pair_spec,
            pair_spec,
            pl.BlockSpec((KV_HEADS, GROUP_COLS), lambda h: (0, 0)),
        ],
        out_shape=[
            jax.ShapeDtypeStruct((TOK, HEADS * HEAD_DIM), jnp.bfloat16),
            jax.ShapeDtypeStruct((TOK, HEADS * HEAD_DIM), jnp.bfloat16),
            jax.ShapeDtypeStruct(pair_shape, jnp.float32),
            jax.ShapeDtypeStruct(pair_shape, jnp.bfloat16),
            jax.ShapeDtypeStruct(pair_shape, jnp.bfloat16),
            jax.ShapeDtypeStruct(pair_shape, jnp.bfloat16),
            jax.ShapeDtypeStruct((KV_HEADS, GROUP_COLS), jnp.float32),
        ],
        scratch_shapes=[
            pltpu.VMEM((WIN, TOK), jnp.float32),
            pltpu.VMEM((WIN, GROUP_COLS), jnp.float32),
            pltpu.VMEM((WIN, GROUP_COLS), jnp.float32),
            pltpu.VMEM((WIN, GROUP_COLS), jnp.bfloat16),
            pltpu.VMEM((WIN, GROUP_COLS), jnp.bfloat16),
        ],
        compiler_params=pltpu.CompilerParams(
            dimension_semantics=("arbitrary",), vmem_limit_bytes=20 << 20
        ),
        cost_estimate=pl.CostEstimate(
            flops=10 * HEADS * TOK * WIN * HEAD_DIM,
            transcendentals=HEADS * TOK * WIN,
            bytes_accessed=8 << 20,
        ),
        name="attention",
    )(marks, sink_logits, bias, queries, cotangent, *packs)


def body(queries, key_rows, value_rows, cotangent, sink_logits, run_lengths, segment_ids):
    n_ctx = lax.axis_size(CTX)
    ctx_index = lax.axis_index(CTX)
    segments = segment_ids[0]
    mark_rows = jnp.broadcast_to(
        segments.astype(jnp.bfloat16)[None, None, :], (8, KV_HEADS, TOK)
    ).reshape(8, KV_COLS)
    own = jnp.concatenate([key_rows[0], value_rows[0], mark_rows], axis=0)
    own = lax.optimization_barrier(own)

    packs = [own] + [None] * (MOST - 1)
    packs[1] = passed_along(own, 1)
    for by in (6, 4, 2):
        packs[by] = passed_along(own, by)
    for by in (6, 4, 2):
        packs[by + 1] = passed_along(packs[1], by)

    run_ends = jnp.cumsum(run_lengths[0])
    before = run_ends <= ctx_index
    run_start = jnp.max(jnp.where(before, run_ends, 0))
    first_mark = segments[0]
    first_count = jnp.sum((segments == first_mark).astype(jnp.int32))
    marks = jnp.stack([ctx_index - run_start, first_mark, first_count]).astype(jnp.int32)
    positions = jnp.arange(TOK, dtype=jnp.int32)
    seen = (segments[:, None] == segments[None, :]) & (
        positions[:, None] <= positions[None, :]
    )
    bias = jnp.where(seen, 0.0, -jnp.inf).astype(jnp.float32)

    attended, grad_query, near, far2, far4, far6, sink_rows = attention(
        marks, sink_logits, bias, queries[0], cotangent[0], packs
    )
    returned = []
    for by, far in ((6, far6), (4, far4), (2, far2)):
        returned.append(passed_along(far, -by))
    grad_sink = -jnp.sum(sink_rows.reshape(HEADS, TOK), axis=1)
    grad_sink = lax.psum(grad_sink, ("ctx_2", "dp_0"))
    near = near + sum(part.astype(jnp.float32) for part in returned)
    last = passed_along(near[2 * TOK :].astype(jnp.bfloat16), -1)
    grad_sink, _ = lax.optimization_barrier((grad_sink, near))
    grad_sink = lax.psum(grad_sink, "ctx_0")
    grad_sink = lax.psum(grad_sink, "ctx_1")
    grad_sink = lax.psum(grad_sink, "dp_1")
    grad_kv = (near[: 2 * TOK] + last.astype(jnp.float32)).astype(jnp.bfloat16)
    scale_down = 1.0 / math.sqrt(lax.axis_size(DP) * n_ctx * TOK)
    return (
        attended[None],
        grad_query[None],
        grad_kv[:TOK][None],
        grad_kv[TOK:][None],
        grad_sink * scale_down,
    )


def solution(mesh):
    split = Mesh(mesh.devices.reshape(8, 2, 8, 4, 2), ("dp_0", "dp_1", "ctx_0", "ctx_1", "ctx_2"))
    in_specs = (
        P(DP, CTX, None),
        P(DP, CTX, None),
        P(DP, CTX, None),
        P(DP, CTX, None),
        P(),
        P(DP, None),
        P(DP, CTX),
    )
    out_specs = (P(DP, CTX, None), P(DP, CTX, None), P(DP, CTX, None), P(DP, CTX, None), P())
    return jax.shard_map(body, mesh=split, in_specs=in_specs, out_specs=out_specs, check_vma=False)
```

```python
import functools
import math

import jax
import jax.numpy as jnp
from jax import lax
from jax.experimental import pallas as pl
from jax.experimental.pallas import tpu as pltpu
from jax.sharding import Mesh
from jax.sharding import PartitionSpec as P


HEADS = 16
KV_HEADS = 4
HEAD_DIM = 128
GROUP = HEADS // KV_HEADS
TOK = 128
MOST = 8
KV_COLS = KV_HEADS * HEAD_DIM
PACK_ROWS = 2 * TOK + 8
WIN = MOST * TOK
GROUP_COLS = GROUP * HEAD_DIM
Z_MEMBERS = 16
PLANE_MEMBERS = 64
CHUNKS = 2
CHUNK_HEADS = KV_HEADS // CHUNKS
CHUNK_COLS = CHUNK_HEADS * HEAD_DIM
FACTOR = HEAD_DIM ** (-0.5)
CTX = ("ctx_0", "ctx_1", "ctx_2")
DP = ("dp_0", "dp_1")


NT = (((1,), (1,)), ((), ()))
NN = (((1,), (0,)), ((), ()))


def passed_along(array, by):
    devices = lax.axis_size(CTX)
    pairs = [(i, i + by) for i in range(devices) if 0 <= i + by < devices]
    return lax.ppermute(array, CTX, pairs)


def dot(left, right, dims):
    return lax.dot_general(left, right, dims, preferred_element_type=jnp.float32)


def attention_kernel(
    fresh,
    first_head,
    place_ref,
    runs_ref,
    sink_ref,
    marks_ref,
    query_ref,
    grad_ref,
    *refs,
):
    packs = refs[:MOST]
    sink_in_ref = None if fresh else refs[MOST + 2]
    refs = refs[MOST:] if fresh else refs[MOST + 3 :]
    (out_ref, grad_query_ref, near_ref, far2_ref, far4_ref, far6_ref, sink_grad_ref) = refs[:7]
    mask_ref, score_ref, cross_ref, weight_ref, slope_ref = refs[7:]
    step = pl.program_id(0)

    @pl.when(step == 0)
    def _():
        if fresh:
            sink_grad_ref[...] = jnp.zeros_like(sink_grad_ref)
        else:
            sink_grad_ref[...] = sink_in_ref[...]
        place = place_ref[0]
        ends = jnp.int32(0)
        run_start = jnp.int32(0)
        for run in range(runs_ref.shape[0]):
            ends = ends + runs_ref[run]
            run_start = jnp.where(ends <= place, ends, run_start)
        reach = place - run_start
        rows = lax.broadcasted_iota(jnp.int32, (TOK, TOK), 0)
        cols = lax.broadcasted_iota(jnp.int32, (TOK, TOK), 1)
        marks = marks_ref[...].astype(jnp.float32)
        wide = jnp.broadcast_to(marks, (TOK, TOK))
        seen = (wide.T == wide) & (rows <= cols)
        mask_ref[:TOK, :] = jnp.where(seen, 0.0, -jnp.inf)
        first_mark = marks[:, :1]
        first_part = wide == jnp.broadcast_to(first_mark, (TOK, TOK))
        for slot in range(1, MOST):
            row = packs[slot][2 * TOK : 2 * TOK + 8, :].astype(jnp.float32)[:1, :]
            same = jnp.sum((row == first_mark).astype(jnp.float32), axis=1, keepdims=True)
            same = jnp.where(slot <= reach, same, 0.0)
            seen = (rows >= TOK - same.astype(jnp.int32)) & first_part
            mask_ref[slot * TOK : (slot + 1) * TOK, :] = jnp.where(seen, 0.0, -jnp.inf)

    def stacked(ref):
        return jnp.concatenate(
            [ref[:, g * HEAD_DIM : (g + 1) * HEAD_DIM] for g in range(GROUP)], axis=0
        )

    query = stacked(query_ref)
    grad = stacked(grad_ref)
    keys = jnp.concatenate([pack[:TOK, :] for pack in packs], axis=0)
    values = jnp.concatenate([pack[TOK : 2 * TOK, :] for pack in packs], axis=0)
    score_ref[...] = dot(keys, query, NT)
    cross_ref[...] = dot(values, grad, NT)
    blocks = [slice(slot * TOK, (slot + 1) * TOK) for slot in range(MOST)]
    lanes = [slice(g * TOK, (g + 1) * TOK) for g in range(GROUP)]
    sink_weights = []
    for g in range(GROUP):
        sink = sink_ref[step * GROUP + g]
        best = jnp.full((8, TOK), sink, jnp.float32)
        for rows in blocks:
            scores = score_ref[rows, lanes[g]] * FACTOR + mask_ref[rows, :]
            score_ref[rows, lanes[g]] = scores
            best = jnp.maximum(best, jnp.max(scores.reshape(TOK // 8, 8, TOK), axis=0))
        top = jnp.max(best, axis=0, keepdims=True)
        total = jnp.zeros((8, TOK), jnp.float32)
        for rows in blocks:
            terms = jnp.exp(score_ref[rows, lanes[g]] - top)
            score_ref[rows, lanes[g]] = terms
            total = total + jnp.sum(terms.reshape(TOK // 8, 8, TOK), axis=0)
        sink_exp = jnp.exp(sink - top)
        scale = 1.0 / (jnp.sum(total, axis=0, keepdims=True) + sink_exp)
        for rows in blocks:
            weights = score_ref[rows, lanes[g]] * scale
            score_ref[rows, lanes[g]] = weights
            weight_ref[rows, lanes[g]] = weights.astype(jnp.bfloat16)
        sink_weights.append(sink_exp * scale)
    out_t = dot(values.T, weight_ref[...], NN).astype(jnp.bfloat16)
    grad_t = grad.T
    row_dot = jnp.sum(grad_t.astype(jnp.float32) * out_t.astype(jnp.float32), axis=0, keepdims=True)
    for g in range(GROUP):
        here = row_dot[:, lanes[g]]
        for rows in blocks:
            slope_ref[rows, lanes[g]] = (
                score_ref[rows, lanes[g]] * (cross_ref[rows, lanes[g]] - here)
            ).astype(jnp.bfloat16)
    head_lane = lax.broadcasted_iota(jnp.int32, (1, TOK), 1) - (first_head + step * GROUP)
    sink_row = jnp.zeros((1, TOK), jnp.float32)
    for g in range(GROUP):
        part = jnp.sum(sink_weights[g] * row_dot[:, lanes[g]], axis=1, keepdims=True)
        sink_row = sink_row - jnp.where(head_lane == g, part, 0.0)
    sink_grad_ref[...] = sink_grad_ref[...] + sink_row
    out = out_t.T
    grad_query = (dot(keys.T, slope_ref[...], NN) * FACTOR).astype(jnp.bfloat16).T
    for g in range(GROUP):
        cols = slice(g * HEAD_DIM, (g + 1) * HEAD_DIM)
        out_ref[:, cols] = out[lanes[g], :]
        grad_query_ref[:, cols] = grad_query[lanes[g], :]
    grad_key = dot(slope_ref[...], query, NN) * FACTOR
    grad_value = dot(weight_ref[...], grad, NN)
    for slot, (ref, half) in enumerate(
        [
            (near_ref, 0),
            (near_ref, 1),
            (far2_ref, 0),
            (far2_ref, 1),
            (far4_ref, 0),
            (far4_ref, 1),
            (far6_ref, 0),
            (far6_ref, 1),
        ]
    ):
        start = half * 2 * TOK
        ref[start : start + TOK, :] = grad_key[blocks[slot], :].astype(ref.dtype)
        ref[start + TOK : start + 2 * TOK, :] = grad_value[blocks[slot], :].astype(ref.dtype)


def attention(chunk, place, runs, sink_logits, marks, queries, cotangent, packs, written):
    first = chunk * CHUNK_HEADS
    wide = pl.BlockSpec((TOK, GROUP_COLS), lambda h: (0, first + h))
    whole_pack = pl.BlockSpec((PACK_ROWS, HEAD_DIM), lambda h: (0, first + h))
    chunk_pack = pl.BlockSpec((PACK_ROWS, HEAD_DIM), lambda h: (0, h))
    pair_spec = pl.BlockSpec((4 * TOK, HEAD_DIM), lambda h: (0, h))
    smem = pl.BlockSpec(memory_space=pltpu.SMEM)
    pair_shape = (4 * TOK, CHUNK_COLS)
    heads = CHUNK_HEADS * GROUP
    sink_spec = pl.BlockSpec((Z_MEMBERS, TOK), lambda h: (0, 0))
    n_fixed = 6 + MOST
    return pl.pallas_call(
        functools.partial(attention_kernel, not written, first * GROUP),
        grid=(CHUNK_HEADS,),
        in_specs=[smem, smem, smem, pl.BlockSpec((1, TOK), lambda h: (0, 0)), wide, wide]
        + [chunk_pack if pack.shape[1] == CHUNK_COLS else whole_pack for pack in packs]
        + ([pl.BlockSpec(memory_space=pl.ANY)] * 2 + [sink_spec] if written else []),
        out_specs=[
            wide,
            wide,
            pair_spec,
            pair_spec,
            pair_spec,
            pair_spec,
            sink_spec,
        ],
        out_shape=[
            jax.ShapeDtypeStruct((TOK, HEADS * HEAD_DIM), jnp.bfloat16),
            jax.ShapeDtypeStruct((TOK, HEADS * HEAD_DIM), jnp.bfloat16),
            jax.ShapeDtypeStruct(pair_shape, jnp.float32),
            jax.ShapeDtypeStruct(pair_shape, jnp.bfloat16),
            jax.ShapeDtypeStruct(pair_shape, jnp.bfloat16),
            jax.ShapeDtypeStruct(pair_shape, jnp.bfloat16),
            jax.ShapeDtypeStruct((Z_MEMBERS, TOK), jnp.float32),
        ],
        scratch_shapes=[
            pltpu.VMEM((WIN, TOK), jnp.float32),
            pltpu.VMEM((WIN, GROUP_COLS), jnp.float32),
            pltpu.VMEM((WIN, GROUP_COLS), jnp.float32),
            pltpu.VMEM((WIN, GROUP_COLS), jnp.bfloat16),
            pltpu.VMEM((WIN, GROUP_COLS), jnp.bfloat16),
        ],
        input_output_aliases={n_fixed: 0, n_fixed + 1: 1} if written else {},
        compiler_params=pltpu.CompilerParams(
            dimension_semantics=("arbitrary",), vmem_limit_bytes=20 << 20
        ),
        cost_estimate=pl.CostEstimate(
            flops=10 * heads * TOK * WIN * HEAD_DIM,
            transcendentals=heads * TOK * WIN,
            bytes_accessed=4 << 20,
        ),
    )(
        place,
        runs,
        lax.slice(sink_logits, (first * GROUP,), (first * GROUP + heads,)),
        marks,
        queries,
        cotangent,
        *packs,
        *written,
    )


def exchanged(spread, axes):
    return jnp.sum(lax.all_to_all(spread, axes, 0, 0, tiled=True), axis=0)


def body(queries, key_rows, value_rows, cotangent, sink_logits, run_lengths, segment_ids):
    n_ctx = lax.axis_size(CTX)
    place = lax.axis_index(CTX).astype(jnp.int32).reshape(1)
    place, segment_ids = lax.optimization_barrier((place, segment_ids))
    mark_rows = jnp.broadcast_to(
        segment_ids[0].astype(jnp.bfloat16)[None, None, :], (8, KV_HEADS, TOK)
    ).reshape(8, KV_COLS)

    def packed(start, stop):
        parts = (key_rows[0], value_rows[0], mark_rows)
        return jnp.concatenate([part[:, start:stop] for part in parts], axis=0)

    near_odd = []
    for chunk in range(CHUNKS):
        mine = packed(chunk * CHUNK_COLS, (chunk + 1) * CHUNK_COLS)
        near_odd.append(passed_along(mine, 1))
    own = packed(0, KV_COLS)
    evens = {0: own}
    for by in (6, 4, 2):
        evens[by] = passed_along(own, by)
    outs = ()
    sinks = ()
    kept = []
    returned = []
    for chunk in range(CHUNKS):
        odds = {1: near_odd[chunk]}
        for by in (6, 4, 2):
            odds[by + 1] = passed_along(near_odd[chunk], by)
        packs = [(odds if slot % 2 else evens)[slot] for slot in range(MOST)]
        *outs, near, far2, far4, far6, sinks = attention(
            chunk,
            place,
            run_lengths[0],
            sink_logits,
            segment_ids,
            queries[0],
            cotangent[0],
            packs,
            (*outs, sinks) if outs else (),
        )
        kept.append(near)
        back = []
        for by, far in ((6, far6), (4, far4), (2, far2)):
            back.append(passed_along(far, -by))
        returned.append(back)
    attended, grad_query = outs
    grad_sink = exchanged(sinks, ("ctx_2", "dp_0"))
    grad_kv = []
    for chunk in range(CHUNKS):
        near = kept[chunk] + sum(part.astype(jnp.float32) for part in returned[chunk])
        last = passed_along(near[2 * TOK :].astype(jnp.bfloat16), -1)
        grad_kv.append((near[: 2 * TOK] + last.astype(jnp.float32)).astype(jnp.bfloat16))
    spread = jnp.broadcast_to(grad_sink[None], (PLANE_MEMBERS, TOK))
    grad_sink = exchanged(spread, ("ctx_0", "ctx_1", "dp_1"))[:HEADS]
    grad_kv = jnp.concatenate(grad_kv, axis=1)
    scale_down = 1.0 / math.sqrt(lax.axis_size(DP) * n_ctx * TOK)
    return (
        attended[None],
        grad_query[None],
        grad_kv[:TOK][None],
        grad_kv[TOK:][None],
        grad_sink * scale_down,
    )


def solution(mesh):
    split = Mesh(mesh.devices.reshape(8, 2, 8, 4, 2), ("dp_0", "dp_1", "ctx_0", "ctx_1", "ctx_2"))
    in_specs = (
        P(DP, CTX, None),
        P(DP, CTX, None),
        P(DP, CTX, None),
        P(DP, CTX, None),
        P(),
        P(DP, None),
        P(DP, CTX),
    )
    out_specs = (P(DP, CTX, None), P(DP, CTX, None), P(DP, CTX, None), P(DP, CTX, None), P())
    return jax.shard_map(body, mesh=split, in_specs=in_specs, out_specs=out_specs, check_vma=False)
```

```python
import functools
import math

import jax
import jax.numpy as jnp
from jax import lax
from jax.experimental import pallas as pl
from jax.experimental.pallas import tpu as pltpu
from jax.sharding import Mesh
from jax.sharding import PartitionSpec as P


HEADS = 16
KV_HEADS = 4
HEAD_DIM = 128
GROUP = HEADS // KV_HEADS
TOK = 128
MOST = 8
KV_COLS = KV_HEADS * HEAD_DIM
PACK_ROWS = 2 * TOK + 8
WIN = MOST * TOK
GROUP_COLS = GROUP * HEAD_DIM
Z_MEMBERS = 16
PLANE_MEMBERS = 64
CHUNKS = 2
CHUNK_HEADS = KV_HEADS // CHUNKS
CHUNK_COLS = CHUNK_HEADS * HEAD_DIM
FACTOR = HEAD_DIM ** (-0.5)
CTX = ("ctx_0", "ctx_1", "ctx_2")
DP = ("dp_0", "dp_1")


NT = (((1,), (1,)), ((), ()))
NN = (((1,), (0,)), ((), ()))


def passed_along(array, by):
    devices = lax.axis_size(CTX)
    pairs = [(i, i + by) for i in range(devices) if 0 <= i + by < devices]
    return lax.ppermute(array, CTX, pairs)


def dot(left, right, dims):
    return lax.dot_general(left, right, dims, preferred_element_type=jnp.float32)


def attention_kernel(
    fresh,
    first_head,
    place_ref,
    runs_ref,
    sink_ref,
    marks_ref,
    query_ref,
    grad_ref,
    *refs,
):
    packs = refs[:MOST]
    sink_in_ref = None if fresh else refs[MOST + 6]
    refs = refs[MOST:] if fresh else refs[MOST + 7 :]
    (out_ref, grad_query_ref, near_ref, far2_ref, far4_ref, far6_ref, sink_grad_ref) = refs[:7]
    mask_ref, score_ref, cross_ref, weight_ref, slope_ref = refs[7:]
    step = pl.program_id(0)

    @pl.when(step == 0)
    def _():
        if fresh:
            sink_grad_ref[...] = jnp.zeros_like(sink_grad_ref)
        else:
            sink_grad_ref[...] = sink_in_ref[...]
        place = place_ref[0]
        ends = jnp.int32(0)
        run_start = jnp.int32(0)
        for run in range(runs_ref.shape[0]):
            ends = ends + runs_ref[run]
            run_start = jnp.where(ends <= place, ends, run_start)
        reach = place - run_start
        rows = lax.broadcasted_iota(jnp.int32, (TOK, TOK), 0)
        cols = lax.broadcasted_iota(jnp.int32, (TOK, TOK), 1)
        marks = marks_ref[...].astype(jnp.float32)
        wide = jnp.broadcast_to(marks, (TOK, TOK))
        seen = (wide.T == wide) & (rows <= cols)
        mask_ref[:TOK, :] = jnp.where(seen, 0.0, -jnp.inf)
        first_mark = marks[:, :1]
        first_part = wide == jnp.broadcast_to(first_mark, (TOK, TOK))
        for slot in range(1, MOST):
            row = packs[slot][2 * TOK : 2 * TOK + 8, :].astype(jnp.float32)[:1, :]
            same = jnp.sum((row == first_mark).astype(jnp.float32), axis=1, keepdims=True)
            same = jnp.where(slot <= reach, same, 0.0)
            seen = (rows >= TOK - same.astype(jnp.int32)) & first_part
            mask_ref[slot * TOK : (slot + 1) * TOK, :] = jnp.where(seen, 0.0, -jnp.inf)

    def stacked(ref):
        return jnp.concatenate(
            [ref[:, g * HEAD_DIM : (g + 1) * HEAD_DIM] for g in range(GROUP)], axis=0
        )

    query = stacked(query_ref)
    grad = stacked(grad_ref)
    keys = jnp.concatenate([pack[:TOK, :] for pack in packs], axis=0)
    values = jnp.concatenate([pack[TOK : 2 * TOK, :] for pack in packs], axis=0)
    score_ref[...] = dot(keys, query, NT)
    cross_ref[...] = dot(values, grad, NT)
    blocks = [slice(slot * TOK, (slot + 1) * TOK) for slot in range(MOST)]
    lanes = [slice(g * TOK, (g + 1) * TOK) for g in range(GROUP)]
    sink_weights = []
    for g in range(GROUP):
        sink = sink_ref[step * GROUP + g]
        best = jnp.full((8, TOK), sink, jnp.float32)
        for rows in blocks:
            scores = score_ref[rows, lanes[g]] * FACTOR + mask_ref[rows, :]
            score_ref[rows, lanes[g]] = scores
            best = jnp.maximum(best, jnp.max(scores.reshape(TOK // 8, 8, TOK), axis=0))
        top = jnp.max(best, axis=0, keepdims=True)
        total = jnp.zeros((8, TOK), jnp.float32)
        for rows in blocks:
            terms = jnp.exp(score_ref[rows, lanes[g]] - top)
            score_ref[rows, lanes[g]] = terms
            total = total + jnp.sum(terms.reshape(TOK // 8, 8, TOK), axis=0)
        sink_exp = jnp.exp(sink - top)
        scale = 1.0 / (jnp.sum(total, axis=0, keepdims=True) + sink_exp)
        for rows in blocks:
            weights = score_ref[rows, lanes[g]] * scale
            score_ref[rows, lanes[g]] = weights
            weight_ref[rows, lanes[g]] = weights.astype(jnp.bfloat16)
        sink_weights.append(sink_exp * scale)
    out_t = dot(values.T, weight_ref[...], NN).astype(jnp.bfloat16)
    grad_t = grad.T
    row_dot = jnp.sum(grad_t.astype(jnp.float32) * out_t.astype(jnp.float32), axis=0, keepdims=True)
    for g in range(GROUP):
        here = row_dot[:, lanes[g]]
        for rows in blocks:
            slope_ref[rows, lanes[g]] = (
                score_ref[rows, lanes[g]] * (cross_ref[rows, lanes[g]] - here)
            ).astype(jnp.bfloat16)
    head_lane = lax.broadcasted_iota(jnp.int32, (1, TOK), 1) - (first_head + step * GROUP)
    sink_row = jnp.zeros((1, TOK), jnp.float32)
    for g in range(GROUP):
        part = jnp.sum(sink_weights[g] * row_dot[:, lanes[g]], axis=1, keepdims=True)
        sink_row = sink_row - jnp.where(head_lane == g, part, 0.0)
    sink_grad_ref[...] = sink_grad_ref[...] + sink_row
    out = out_t.T
    grad_query = (dot(keys.T, slope_ref[...], NN) * FACTOR).astype(jnp.bfloat16).T
    for g in range(GROUP):
        cols = slice(g * HEAD_DIM, (g + 1) * HEAD_DIM)
        out_ref[:, cols] = out[lanes[g], :]
        grad_query_ref[:, cols] = grad_query[lanes[g], :]
    grad_key = dot(slope_ref[...], query, NN) * FACTOR
    grad_value = dot(weight_ref[...], grad, NN)
    for slot, (ref, half) in enumerate(
        [
            (near_ref, 0),
            (near_ref, 1),
            (far2_ref, 0),
            (far2_ref, 1),
            (far4_ref, 0),
            (far4_ref, 1),
            (far6_ref, 0),
            (far6_ref, 1),
        ]
    ):
        start = half * 2 * TOK
        ref[start : start + TOK, :] = grad_key[blocks[slot], :].astype(ref.dtype)
        ref[start + TOK : start + 2 * TOK, :] = grad_value[blocks[slot], :].astype(ref.dtype)


def attention(chunk, place, runs, sink_logits, marks, queries, cotangent, packs, written):
    first = chunk * CHUNK_HEADS
    wide = pl.BlockSpec((TOK, GROUP_COLS), lambda h: (0, first + h))
    whole_pack = pl.BlockSpec((PACK_ROWS, HEAD_DIM), lambda h: (0, first + h))
    chunk_pack = pl.BlockSpec((PACK_ROWS, HEAD_DIM), lambda h: (0, h))
    pair_spec = pl.BlockSpec((4 * TOK, HEAD_DIM), lambda h: (0, first + h))
    smem = pl.BlockSpec(memory_space=pltpu.SMEM)
    pair_shape = (4 * TOK, KV_COLS)
    heads = CHUNK_HEADS * GROUP
    sink_spec = pl.BlockSpec((Z_MEMBERS, TOK), lambda h: (0, 0))
    n_fixed = 6 + MOST
    return pl.pallas_call(
        functools.partial(attention_kernel, not written, first * GROUP),
        grid=(CHUNK_HEADS,),
        in_specs=[smem, smem, smem, pl.BlockSpec((1, TOK), lambda h: (0, 0)), wide, wide]
        + [chunk_pack if pack.shape[1] == CHUNK_COLS else whole_pack for pack in packs]
        + ([pl.BlockSpec(memory_space=pl.ANY)] * 6 + [sink_spec] if written else []),
        out_specs=[
            wide,
            wide,
            pair_spec,
            pair_spec,
            pair_spec,
            pair_spec,
            sink_spec,
        ],
        out_shape=[
            jax.ShapeDtypeStruct((TOK, HEADS * HEAD_DIM), jnp.bfloat16),
            jax.ShapeDtypeStruct((TOK, HEADS * HEAD_DIM), jnp.bfloat16),
            jax.ShapeDtypeStruct(pair_shape, jnp.float32),
            jax.ShapeDtypeStruct(pair_shape, jnp.bfloat16),
            jax.ShapeDtypeStruct(pair_shape, jnp.bfloat16),
            jax.ShapeDtypeStruct(pair_shape, jnp.bfloat16),
            jax.ShapeDtypeStruct((Z_MEMBERS, TOK), jnp.float32),
        ],
        scratch_shapes=[
            pltpu.VMEM((WIN, TOK), jnp.float32),
            pltpu.VMEM((WIN, GROUP_COLS), jnp.float32),
            pltpu.VMEM((WIN, GROUP_COLS), jnp.float32),
            pltpu.VMEM((WIN, GROUP_COLS), jnp.bfloat16),
            pltpu.VMEM((WIN, GROUP_COLS), jnp.bfloat16),
        ],
        input_output_aliases={n_fixed + out: out for out in range(6)} if written else {},
        compiler_params=pltpu.CompilerParams(
            dimension_semantics=("arbitrary",), vmem_limit_bytes=20 << 20
        ),
        cost_estimate=pl.CostEstimate(
            flops=10 * heads * TOK * WIN * HEAD_DIM,
            transcendentals=heads * TOK * WIN,
            bytes_accessed=4 << 20,
        ),
    )(
        place,
        runs,
        lax.slice(sink_logits, (first * GROUP,), (first * GROUP + heads,)),
        marks,
        queries,
        cotangent,
        *packs,
        *written,
    )


def exchanged(spread, axes):
    return jnp.sum(lax.all_to_all(spread, axes, 0, 0, tiled=True), axis=0)


def body(queries, key_rows, value_rows, cotangent, sink_logits, run_lengths, segment_ids):
    n_ctx = lax.axis_size(CTX)
    place = lax.axis_index(CTX).astype(jnp.int32).reshape(1)
    place, segment_ids = lax.optimization_barrier((place, segment_ids))
    mark_rows = jnp.broadcast_to(
        segment_ids[0].astype(jnp.bfloat16)[None, None, :], (8, KV_HEADS, TOK)
    ).reshape(8, KV_COLS)

    def packed(start, stop):
        parts = (key_rows[0], value_rows[0], mark_rows)
        return jnp.concatenate([part[:, start:stop] for part in parts], axis=0)

    near_odd = []
    for chunk in range(CHUNKS):
        mine = packed(chunk * CHUNK_COLS, (chunk + 1) * CHUNK_COLS)
        near_odd.append(passed_along(mine, 1))
    own = packed(0, KV_COLS)
    evens = {0: own}
    for by in (6, 4, 2):
        evens[by] = passed_along(own, by)
    outs = ()
    for chunk in range(CHUNKS):
        odds = {1: near_odd[chunk]}
        for by in (6, 4, 2):
            odds[by + 1] = passed_along(near_odd[chunk], by)
        packs = [(odds if slot % 2 else evens)[slot] for slot in range(MOST)]
        outs = attention(
            chunk,
            place,
            run_lengths[0],
            sink_logits,
            segment_ids,
            queries[0],
            cotangent[0],
            packs,
            tuple(outs),
        )
    attended, grad_query, near, far2, far4, far6, sinks = outs
    returned = []
    for by, far in ((6, far6), (4, far4), (2, far2)):
        returned.append(passed_along(far, -by))
    grad_sink = exchanged(sinks, ("ctx_2", "dp_0"))
    near = near + sum(part.astype(jnp.float32) for part in returned)
    last = passed_along(near[2 * TOK :].astype(jnp.bfloat16), -1)
    grad_kv = (near[: 2 * TOK] + last.astype(jnp.float32)).astype(jnp.bfloat16)
    spread = jnp.broadcast_to(grad_sink[None], (PLANE_MEMBERS, TOK))
    grad_sink = exchanged(spread, ("ctx_0", "ctx_1", "dp_1"))[:HEADS]
    scale_down = 1.0 / math.sqrt(lax.axis_size(DP) * n_ctx * TOK)
    return (
        attended[None],
        grad_query[None],
        grad_kv[:TOK][None],
        grad_kv[TOK:][None],
        grad_sink * scale_down,
    )


def solution(mesh):
    split = Mesh(mesh.devices.reshape(8, 2, 8, 4, 2), ("dp_0", "dp_1", "ctx_0", "ctx_1", "ctx_2"))
    in_specs = (
        P(DP, CTX, None),
        P(DP, CTX, None),
        P(DP, CTX, None),
        P(DP, CTX, None),
        P(),
        P(DP, None),
        P(DP, CTX),
    )
    out_specs = (P(DP, CTX, None), P(DP, CTX, None), P(DP, CTX, None), P(DP, CTX, None), P())
    return jax.shard_map(body, mesh=split, in_specs=in_specs, out_specs=out_specs, check_vma=False)
```
